256 devices in a mesh: section: 2 (over y_lo), dp: 16 (over z, y_hi), tensor: 8 (over x, core).
Axes of the slice: x: 4, y: 4 (y_hi: 2, y_lo: 2; y = y_hi * 2 + y_lo), z: 8, core: 2. Of those that a mesh axis runs over, the one named last changes fastest.
Arguments:
- fwd_in: bfloat16 [2, 1024, 8192], P('section', 'tensor', 'dp'), may hold values from -6 to 6
- grad_in: bfloat16 [2, 1024, 8192], P('section', 'tensor', 'dp'), may hold values from -6 to 6
- saved_gate: bfloat16 [2, 1024, 14336], P('section', 'dp', 'tensor'), may hold values from -8 to 8
- saved_up: bfloat16 [2, 1024, 14336], P('section', 'dp', 'tensor'), may hold values from -6 to 6
- gate_weight: bfloat16 [2, 8192, 14336], P('section', 'dp', 'tensor'), may hold values from -0.0625 to 0.0625
- up_weight: bfloat16 [2, 8192, 14336], P('section', 'dp', 'tensor'), may hold values from -0.0625 to 0.0625
- down_weight: bfloat16 [2, 14336, 8192], P('section', 'tensor', 'dp'), may hold values from -0.046875 to 0.046875
Outputs:
- fwd_out: bfloat16 [2, 1024, 8192], P('section', 'tensor', 'dp')
- bwd_out: bfloat16 [2, 1024, 8192], P('section', 'tensor', 'dp')
- handed: bfloat16 [2, 1024, 8192], P('section', 'tensor', 'dp')
The draws below stay inside these ranges and needn't reach their ends.
All inputs are finite; a program needn't handle non-finite values.
Results may differ from the reference program's by a relative error of at most 0.022.
Values may be sent and summed in bfloat16 or wider, within the bound.
No kernel may reach another device: no remote copies, remote signals or barrier semaphores. Data moves between devices by JAX's collectives and lax.ppermute only.
A program may use at most 128 MiB of HBM per device.

```python
import jax
import jax.numpy as jnp
from jax import lax

D = 8192
FF = 14336
SECTIONS = 2
TOKENS = 1024
N_DP = 16


def levels(stream_key, shape, shards, smallest, largest):
    gain = 1.0
    for axis_at, blocks in shards:
        draws = jax.random.uniform(jax.random.fold_in(jax.random.fold_in(stream_key, 6), axis_at), (blocks,), jnp.float32, smallest / len(shards), largest / len(shards))
        gain = gain * jnp.repeat(jnp.exp(draws), shape[axis_at] // blocks).reshape((-1,) + (1,) * (len(shape) - 1 - axis_at))
    return gain


def gaussian(key, extent, scale, reach, split=(), held_as=jnp.bfloat16):
    entries = jax.random.normal(key, extent, jnp.float32) * scale
    if len(split) > 0:
        entries = levels(key, extent, split, -0.22, 0.18) * entries
    return jnp.clip(entries, min=-reach, max=reach).astype(held_as)


def setup_inputs(seed: int = 0) -> dict:
    splits = jax.random.split(jax.random.key(seed), 8)
    return {
        "fwd_in": gaussian(splits[0], (SECTIONS, TOKENS, D), 1.0, 6.0, ((0, 2), (1, 8), (2, 16))),
        "grad_in": gaussian(splits[1], (SECTIONS, TOKENS, D), 1.0, 6.0, ((0, 2), (1, 8), (2, 16))),
        "saved_gate": gaussian(splits[2], (SECTIONS, TOKENS, FF), 2.0, 8.0, ((0, 2), (1, 16), (2, 8))),
        "saved_up": gaussian(splits[3], (SECTIONS, TOKENS, FF), 1.0, 6.0, ((0, 2), (1, 16), (2, 8))),
        "gate_weight": gaussian(splits[4], (SECTIONS, D, FF), D ** -0.5, 0.0625, ((0, 2), (1, 16), (2, 8))),
        "up_weight": gaussian(splits[5], (SECTIONS, D, FF), D ** -0.5, 0.0625, ((0, 2), (1, 16), (2, 8))),
        "down_weight": gaussian(splits[6], (SECTIONS, FF, D), FF ** -0.5, 0.046875, ((0, 2), (1, 8), (2, 16))),
    }


def blockwise(left, right, contract_right):
    width = D // N_DP

    def step(carry, index):
        start = index * width
        part = lax.dynamic_slice_in_dim(left, start, width, 1)
        weights = lax.dynamic_slice_in_dim(right, start, width, contract_right)
        term = lax.dot_general(part, weights, (((1,), (contract_right,)), ((), ())), preferred_element_type=jnp.float32)
        term = lax.optimization_barrier(term.astype(jnp.bfloat16)).astype(jnp.float32)
        return carry + term, None

    start_sum = jnp.zeros((left.shape[0], right.shape[1 - contract_right]), jnp.float32)
    total, unused = lax.scan(step, start_sum, jnp.arange(N_DP, dtype=jnp.int32))
    return total


def reference(fwd_in, grad_in, saved_gate, saved_up, gate_weight, up_weight, down_weight):
    forward_list = []
    backward_list = []
    for section in range(SECTIONS):
        inputs = fwd_in[section]
        gate = blockwise(inputs, gate_weight[section], 0)
        up = blockwise(inputs, up_weight[section], 0)
        hidden = (jax.nn.silu(gate) * up).astype(jnp.bfloat16)
        mixed = jnp.dot(hidden, down_weight[section], preferred_element_type=jnp.float32)
        forward_list.append((inputs.astype(jnp.float32) + mixed).astype(jnp.bfloat16))
        grads = grad_in[section]
        slope = blockwise(grads, down_weight[section], 1)
        gvals = saved_gate[section].astype(jnp.float32)
        uvals = saved_up[section].astype(jnp.float32)
        sig = jax.nn.sigmoid(gvals)
        gate_grad = (slope * uvals * sig * (1.0 + gvals * (1.0 - sig))).astype(jnp.bfloat16)
        up_grad = (slope * gvals * sig).astype(jnp.bfloat16)
        back = lax.dot_general(gate_grad, gate_weight[section], (((1,), (1,)), ((), ())), preferred_element_type=jnp.float32)
        back = back + lax.dot_general(up_grad, up_weight[section], (((1,), (1,)), ((), ())), preferred_element_type=jnp.float32)
        backward_list.append((grads.astype(jnp.float32) + back).astype(jnp.bfloat16))
    fwd_out = jnp.stack(forward_list)
    bwd_out = jnp.stack(backward_list)
    handed = jnp.stack([bwd_out[1], fwd_out[0]])
    return fwd_out, bwd_out, handed
```

```python
import jax
import jax.numpy as jnp
from jax import lax
from jax.sharding import Mesh
from jax.sharding import PartitionSpec as P

F32 = jnp.float32
BF16 = jnp.bfloat16


def shift(v, axis, by):
    n = lax.axis_size(axis)
    return lax.ppermute(v, axis, [(i, (i + by) % n) for i in range(n)])


def part(v, index, size, dim):
    return lax.dynamic_slice_in_dim(v, index * size, size, dim)


def swap_half(v, dim, me):
    size = v.shape[dim] // 2
    kept = part(v, me, size, dim)
    return kept, shift(part(v, 1 - me, size, dim), "y", 1)


def gather_tensor(v):
    chips = jnp.concatenate(
        [v, shift(v, "x", -1), shift(v, "x", 2), shift(v, "x", 1)], axis=0
    )
    return jnp.concatenate([chips, shift(chips, "c", 1)], axis=0)


def reduce_tensor(v):
    half = v.shape[0] // 2
    rows = half // 4
    v = v[:half] + shift(v[half:].astype(BF16), "c", 1).astype(F32)
    block = [v[j * rows:(j + 1) * rows] for j in range(4)]
    total = block[0]
    for j, by in ((1, 1), (3, -1), (2, 2)):
        total = total + shift(block[j].astype(BF16), "x", by).astype(F32)
    return total


def ring_reduce(block, width):
    def add(left, right):
        return (left.astype(F32) + right.astype(F32)).astype(BF16)

    half = width // 2
    far = block(4)
    up, down = shift(far[:, :half], "z", 1), shift(far[:, half:], "z", -1)
    a, b = block(3), block(-3)
    up = jnp.concatenate([add(a[:, :half], up), a[:, half:]], axis=1)
    down = jnp.concatenate([b[:, :half], add(b[:, half:], down)], axis=1)
    up, down = shift(up, "z", 1), shift(down, "z", -1)
    up, down = shift(add(block(2), up), "z", 1), shift(add(block(-2), down), "z", -1)
    up, down = shift(add(block(1), up), "z", 1), shift(add(block(-1), down), "z", -1)
    return block(0).astype(F32) + up.astype(F32) + down.astype(F32)


def ring_gather(v):
    half = v.shape[1] // 2
    a1, b1 = shift(v, "z", -1), shift(v, "z", 1)
    a2, b2 = shift(a1, "z", -1), shift(b1, "z", 1)
    a3, b3 = shift(a2, "z", -1), shift(b2, "z", 1)
    a4, b4 = shift(a3[:, :half], "z", -1), shift(b3[:, half:], "z", 1)
    return [v, a1, a2, a3, jnp.concatenate([a4, b4], axis=1), b3, b2, b1]


def local(fwd_in, grad_in, saved_gate, saved_up, gate_weight, up_weight, down_weight):
    inputs = fwd_in[0]
    grads = grad_in[0]
    z, y = lax.axis_index("z"), lax.axis_index("y")
    x, c = lax.axis_index("x"), lax.axis_index("c")
    rows, feats = inputs.shape

    def place(k):
        owner = (z + k) % 8
        return 4 * ((owner % 2 + c) % 2) + (owner // 2 + 4 - x) % 4

    grads_pair = jnp.concatenate([grads, shift(grads, "y", 1)], axis=1)
    kept, got = swap_half(down_weight[0], 0, y)
    w_down = jnp.concatenate([kept, got], axis=1)
    inputs_pair = jnp.concatenate([inputs, shift(inputs, "y", 1)], axis=1)
    cols = w_down.shape[0]
    w_both = jnp.stack([gate_weight[0], up_weight[0]])
    kept, got = swap_half(w_both, 2, y)
    w_both = jnp.concatenate(
        [jnp.concatenate([kept[0], kept[1]], axis=1), jnp.concatenate([got[0], got[1]], axis=1)],
        axis=0,
    )
    kept, got = swap_half(jnp.stack([saved_gate[0], saved_up[0]]), 2, y)
    saved = jnp.where(
        y == 0, jnp.concatenate([kept, got], axis=1), jnp.concatenate([got, kept], axis=1)
    ).astype(F32)

    all_grads = gather_tensor(grads_pair)
    all_inputs = gather_tensor(inputs_pair)

    term = lax.dot_general(
        all_grads, w_down, (((1,), (1,)), ((), ())), preferred_element_type=F32
    ).astype(BF16)
    slope = ring_reduce(lambda k: part(term, place(k), rows, 0), cols)

    both = jnp.dot(all_inputs, w_both, preferred_element_type=F32).astype(BF16)
    both = lax.psum_scatter(both, "z", scatter_dimension=0, tiled=True).astype(F32)
    hidden = (jax.nn.silu(both[:, :cols]) * both[:, cols:]).astype(BF16)
    hidden = lax.all_gather(hidden, "z", axis=0, tiled=True)

    gvals, uvals = saved[0], saved[1]
    sig = jax.nn.sigmoid(gvals)
    gate_grad = (slope * uvals * sig * (1.0 + gvals * (1.0 - sig))).astype(BF16)
    up_grad = (slope * gvals * sig).astype(BF16)
    pieces = jnp.zeros((8 * rows, 2 * cols), BF16)
    for k, piece in enumerate(ring_gather(jnp.concatenate([gate_grad, up_grad], axis=1))):
        pieces = lax.dynamic_update_slice_in_dim(pieces, piece, place(k) * rows, 0)
    back = lax.dot_general(pieces, w_both, (((1,), (1,)), ((), ())), preferred_element_type=F32)
    back = reduce_tensor(back)
    back = back[:, :feats] + shift(back[:, feats:].astype(BF16), "y", 1).astype(F32)
    backward_result = (grads.astype(F32) + back).astype(BF16)

    mixed = jnp.dot(hidden, w_down, preferred_element_type=F32)
    mixed = reduce_tensor(mixed)
    mixed = mixed[:, :feats] + shift(mixed[:, feats:].astype(BF16), "y", 1).astype(F32)
    forward_result = (inputs.astype(F32) + mixed).astype(BF16)

    outgoing = jnp.where(lax.axis_index("s") == 0, forward_result, backward_result)
    received = shift(outgoing, "s", 1)
    return (forward_result[None], backward_result[None], received[None])


def solution(mesh):
    fine = Mesh(mesh.devices.reshape(2, 8, 2, 4, 2), ("s", "z", "y", "x", "c"))
    tokens = P("s", ("x", "c"), ("z", "y"))
    hidden = P("s", ("z", "y"), ("x", "c"))
    return jax.shard_map(
        local,
        mesh=fine,
        in_specs=(tokens, tokens, hidden, hidden, hidden, hidden, tokens),
        out_specs=(tokens, tokens, tokens),
        check_vma=False,
    )
```

```python
import jax
import jax.numpy as jnp
from jax import lax
from jax.experimental import pallas as pl
from jax.experimental.layout import Layout, with_layout_constraint
from jax.sharding import Mesh
from jax.sharding import PartitionSpec as P

F32 = jnp.float32
BF16 = jnp.bfloat16


def shift(v, axis, by):
    n = lax.axis_size(axis)
    return lax.ppermute(v, axis, [(i, (i + by) % n) for i in range(n)])


def join(*values):
    return lax.optimization_barrier(values)


def part(v, index, size, dim):
    return lax.dynamic_slice_in_dim(v, index * size, size, dim)


def put(base, piece, row, col=0):
    return lax.dynamic_update_slice(base, piece, (jnp.int32(row), jnp.int32(col)))


def dot(left, right):
    return jnp.dot(left, right, preferred_element_type=F32)


def dot_t(left, right):
    return lax.dot_general(left, right, (((1,), (1,)), ((), ())), preferred_element_type=F32)


def product_kernel(left_ref, right_ref, out_ref):
    out_ref[...] = dot_t(left_ref[...], right_ref[...]).astype(out_ref.dtype)


def slope_product(left, right):
    m, k = left.shape
    n = right.shape[0]
    tile = m // 4
    return pl.pallas_call(
        product_kernel,
        grid=(4,),
        in_specs=[
            pl.BlockSpec((tile, k), lambda i: (i, 0)),
            pl.BlockSpec((n, k), lambda i: (0, 0)),
        ],
        out_specs=pl.BlockSpec((tile, n), lambda i: (i, 0)),
        out_shape=jax.ShapeDtypeStruct((m, n), BF16),
        cost_estimate=pl.CostEstimate(flops=int(4e10), transcendentals=0, bytes_accessed=0),
    )(left, right)


def add(left, right):
    return (left.astype(F32) + right.astype(F32)).astype(BF16)


def both_ways(up, down):
    up, down = join(up, down)
    return shift(up, "z", 1), shift(down, "z", -1)


def reduce_cores(product, away, stay):
    return product(stay) + shift(product(away).astype(BF16), "c", 1).astype(F32)


def reduce_chips(v):
    rows = v.shape[0] // 4
    sends = join(*(v[j * rows:(j + 1) * rows].astype(BF16) for j in (2, 1, 3)))
    total = v[:rows]
    for piece, by in zip(sends, (2, 1, -1)):
        total = total + shift(piece, "x", by).astype(F32)
    return total


def local(fwd_in, grad_in, saved_gate, saved_up, gate_weight, up_weight, down_weight):
    inputs = fwd_in[0]
    grads = grad_in[0]
    w_gate, w_up, w_down = gate_weight[0], up_weight[0], down_weight[0]
    z, y = lax.axis_index("z"), lax.axis_index("y")
    x, c = lax.axis_index("x"), lax.axis_index("c")
    rows, feats = inputs.shape
    cols = w_gate.shape[1] // 2
    cut = 4 * cols // 7

    def owner(k):
        return (z + k + 8) % 8

    def place(k):
        return 4 * ((owner(k) + c) % 2) + (owner(k) // 2 + 4 - x) % 4

    tokens = jnp.stack([inputs, grads])
    w_away = jnp.concatenate([part(w_gate, 1 - y, cols, 1), part(w_up, 1 - y, cols, 1)], axis=1)
    tokens_got = shift(tokens, "y", 1)
    tokens_got, w_away = join(tokens_got, w_away)
    tokens = jnp.concatenate([inputs, tokens_got[0], grads, tokens_got[1]], axis=1)
    (tokens,) = join(lax.all_gather(tokens, ("x", "c"), axis=0, tiled=True))
    w_got = shift(w_away, "y", 1)
    down_away = part(w_down, 1 - y, cols, 0)
    w_both = jnp.zeros((2 * feats, 2 * cols), BF16)
    w_both = put(w_both, part(w_gate, y, cols, 1), 0)
    w_both = put(w_both, part(w_up, y, cols, 1), 0, cols)
    down_kept = part(w_down, y, cols, 0)
    saved = jnp.concatenate([saved_gate[0], saved_up[0]], axis=0)
    saved_away, saved = part(saved, 1 - y, cols, 1), part(saved, y, cols, 1)
    w_got, w_both, down_away, down_kept, saved, saved_away = join(
        w_got, w_both, down_away, down_kept, saved, saved_away
    )

    down_got = shift(down_away, "y", 1)
    (w_both,) = join(put(w_both, w_got, feats))
    both = dot(tokens[:, :2 * feats], w_both)
    both = both.astype(BF16)
    ready = both
    both = lax.psum_scatter(both, "z", scatter_dimension=0, tiled=True)
    saved_got = shift(saved_away, "y", 1)
    half = rows // 2
    saved = jnp.where(
        y == 0,
        jnp.concatenate([saved[:half], saved_got[:half], saved[half:], saved_got[half:]]),
        jnp.concatenate([saved_got[:half], saved[:half], saved_got[half:], saved[half:]]),
    )
    down_got, saved, ready = join(down_got, saved, ready)
    (down_pair,) = join(jnp.concatenate([down_kept, down_got], axis=1))
    term = slope_product(tokens[:, 2 * feats:], down_pair)

    def block(k):
        return part(term, owner(k), rows, 0)

    a = block(4)
    up, down = join(*both_ways(a[:, :cut], a[:, cut:]))
    a, b = block(3), block(-3)
    up = jnp.concatenate([add(a[:, :cut], up), a[:, cut:]], axis=1)
    down = jnp.concatenate([b[:, :cut], add(b[:, cut:], down)], axis=1)
    up, down = join(*both_ways(up, down))
    up, down = join(*both_ways(add(block(2), up), add(block(-2), down)))
    up, down = join(*both_ways(add(block(1), up), add(block(-1), down)))
    slope = block(0).astype(F32) + up.astype(F32) + down.astype(F32)
    gvals, uvals = saved[:rows].astype(F32), saved[rows:].astype(F32)
    sig = jax.nn.sigmoid(gvals)
    gate_grad = (slope * uvals * sig * (1.0 + gvals * (1.0 - sig))).astype(BF16)
    up_grad = (slope * gvals * sig).astype(BF16)
    pieces, both = join(jnp.concatenate([gate_grad, up_grad], axis=1), both)
    pieces = lax.all_gather(pieces, "z", axis=0, tiled=True)
    pieces = with_layout_constraint(pieces, Layout(major_to_minor=(0, 1)))

    both = both.astype(F32)
    hidden = (jax.nn.silu(both[:, :cols]) * both[:, cols:]).astype(BF16)
    spots = put(jnp.zeros((8 * rows, cols), BF16), hidden, place(0) * rows)
    up, down = hidden, hidden
    for k in (1, 2, 3):
        up, down = join(*both_ways(up, down))
        spots = put(put(spots, up, place(-k) * rows), down, place(k) * rows)
    up, down = both_ways(up[:, :cut], down[:, cut:])
    spots = put(put(spots, up, place(4) * rows), down, place(4) * rows, cut)
    mixed = reduce_cores(lambda v: dot(v, down_pair), spots[4 * rows:], spots[:4 * rows])
    pieces, mixed = join(pieces, mixed)

    def chosen(core):
        return jnp.concatenate(
            [part(pieces, 2 * ((x + j) % 4) + core, rows, 0) for j in range(4)], axis=0
        )

    mixed = reduce_chips(mixed)
    back = reduce_cores(lambda v: dot_t(v, w_both), *join(chosen(1 - c), chosen(c)))
    back = reduce_chips(back)
    (ends,) = join(jnp.stack([mixed[:, feats:], back[:, feats:]]).astype(BF16))
    ends = shift(ends, "y", 1).astype(F32)
    forward_result = (inputs.astype(F32) + mixed[:, :feats] + ends[0]).astype(BF16)
    backward_result = (grads.astype(F32) + back[:, :feats] + ends[1]).astype(BF16)

    outgoing = jnp.where(lax.axis_index("s") == 0, forward_result, backward_result)
    received = shift(outgoing, "s", 1)
    return (forward_result[None], backward_result[None], received[None])


def solution(mesh):
    fine = Mesh(mesh.devices.reshape(2, 8, 2, 4, 2), ("s", "z", "y", "x", "c"))
    tokens = P("s", ("x", "c"), ("z", "y"))
    hidden = P("s", ("z", "y"), ("x", "c"))
    return jax.shard_map(
        local,
        mesh=fine,
        in_specs=(tokens, tokens, hidden, hidden, hidden, hidden, tokens),
        out_specs=(tokens, tokens, tokens),
        check_vma=False,
    )
```

```python
import jax
import jax.numpy as jnp
from jax import lax
from jax.experimental import pallas as pl
from jax.experimental.pallas import tpu as pltpu
from jax.experimental.layout import Layout, with_layout_constraint
from jax.sharding import Mesh
from jax.sharding import PartitionSpec as P

F32 = jnp.float32
BF16 = jnp.bfloat16


def shift(v, axis, by):
    n = lax.axis_size(axis)
    return lax.ppermute(v, axis, [(i, (i + by) % n) for i in range(n)])


def join(*values):
    return lax.optimization_barrier(values)


def part(v, index, size, dim):
    return lax.dynamic_slice_in_dim(v, index * size, size, dim)


def put(base, piece, row, col=0):
    return lax.dynamic_update_slice(base, piece, (jnp.int32(row), jnp.int32(col)))


def dot(left, right):
    return jnp.dot(left, right, preferred_element_type=F32)


def dot_t(left, right):
    return lax.dot_general(left, right, (((1,), (1,)), ((), ())), preferred_element_type=F32)


def slope_kernel(left_ref, kept_ref, got_ref, out_ref):
    feats = kept_ref.shape[1]
    total = dot_t(left_ref[:, :feats], kept_ref[...]) + dot_t(left_ref[:, feats:], got_ref[...])
    out_ref[...] = total.astype(out_ref.dtype)


def gate_kernel(left_ref, kept_ref, got_ref, out_ref):
    feats = kept_ref.shape[0]
    total = dot(left_ref[:, :feats], kept_ref[...]) + dot(left_ref[:, feats:], got_ref[...])
    out_ref[...] = total.astype(out_ref.dtype)


def product(kernel, tokens, column, kept, got, width, steps, flops):
    m, k = tokens.shape[0], tokens.shape[1] // 2
    half = got.shape
    return pl.pallas_call(
        kernel,
        grid=(steps,),
        in_specs=[
            pl.BlockSpec((m // steps, k), lambda i: (i, column)),
            pl.BlockSpec(half, lambda i: (0, 0)),
            pl.BlockSpec(half, lambda i: (0, 0)),
        ],
        out_specs=pl.BlockSpec((m // steps, width), lambda i: (i, 0)),
        out_shape=jax.ShapeDtypeStruct((m, width), BF16),
        compiler_params=pltpu.CompilerParams(vmem_limit_bytes=32 << 20),
        cost_estimate=pl.CostEstimate(flops=flops, transcendentals=0, bytes_accessed=0),
    )(tokens, kept, got)


def add(left, right):
    return (left.astype(F32) + right.astype(F32)).astype(BF16)


def both_ways(up, down):
    up, down = join(up, down)
    return shift(up, "z", 1), shift(down, "z", -1)


def reduce_cores(product, away, stay):
    return product(stay) + shift(product(away).astype(BF16), "c", 1).astype(F32)


def reduce_chips(v):
    rows = v.shape[0] // 4
    sends = join(*(v[j * rows:(j + 1) * rows].astype(BF16) for j in (2, 1, 3)))
    total = v[:rows]
    for piece, by in zip(sends, (2, 1, -1)):
        total = total + shift(piece, "x", by).astype(F32)
    return total


def local(fwd_in, grad_in, saved_gate, saved_up, gate_weight, up_weight, down_weight):
    inputs = fwd_in[0]
    grads = grad_in[0]
    w_gate, w_up, w_down = gate_weight[0], up_weight[0], down_weight[0]
    z, y = lax.axis_index("z"), lax.axis_index("y")
    x, c = lax.axis_index("x"), lax.axis_index("c")
    rows, feats = inputs.shape
    cols = w_gate.shape[1] // 2
    cut = 4 * cols // 7

    def owner(k):
        return (z + k + 8) % 8

    def place(k):
        return 4 * ((owner(k) + c) % 2) + (owner(k) // 2 + 4 - x) % 4

    tokens = jnp.stack([inputs, grads])
    w_away = jnp.concatenate([part(w_gate, 1 - y, cols, 1), part(w_up, 1 - y, cols, 1)], axis=1)
    tokens_got = shift(tokens, "y", 1)
    tokens_got, w_away = join(tokens_got, w_away)
    tokens = jnp.concatenate([inputs, tokens_got[0], grads, tokens_got[1]], axis=1)
    (tokens,) = join(lax.all_gather(tokens, ("x", "c"), axis=0, tiled=True))
    w_got = shift(w_away, "y", 1)
    down_away = part(w_down, 1 - y, cols, 0)
    w_both = jnp.zeros((2 * feats, 2 * cols), BF16)
    w_both = put(w_both, part(w_gate, y, cols, 1), 0)
    w_both = put(w_both, part(w_up, y, cols, 1), 0, cols)
    down_kept = part(w_down, y, cols, 0)
    saved = jnp.concatenate([saved_gate[0], saved_up[0]], axis=0)
    saved_away, saved = part(saved, 1 - y, cols, 1), part(saved, y, cols, 1)
    w_got, w_both, down_away, down_kept, saved, saved_away = join(
        w_got, w_both, down_away, down_kept, saved, saved_away
    )

    down_got = shift(down_away, "y", 1)
    both = product(gate_kernel, tokens, 0, w_both, w_got, 2 * cols, 4, int(1.5e10))
    ready = both
    both = lax.psum_scatter(both, "z", scatter_dimension=0, tiled=True)
    saved_got = shift(saved_away, "y", 1)
    half = rows // 2
    saved = jnp.where(
        y == 0,
        jnp.concatenate([saved[:half], saved_got[:half], saved[half:], saved_got[half:]]),
        jnp.concatenate([saved_got[:half], saved[:half], saved_got[half:], saved[half:]]),
    )
    down_got, saved, ready, w_got = join(down_got, saved, ready, w_got)
    term = product(slope_kernel, tokens, 1, down_kept, down_got, cols, 2, int(4e10))

    def block(k):
        return part(term, owner(k), rows, 0)

    a = block(4)
    up, down = both_ways(a[:, :cut], a[:, cut:])
    down_pair = jnp.concatenate([down_kept, down_got], axis=1)
    w_both = put(w_both, w_got, feats)
    up, down, down_pair, w_both = join(up, down, down_pair, w_both)
    a, b = block(3), block(-3)
    up = jnp.concatenate([add(a[:, :cut], up), a[:, cut:]], axis=1)
    down = jnp.concatenate([b[:, :cut], add(b[:, cut:], down)], axis=1)
    up, down = join(*both_ways(up, down))
    up, down = join(*both_ways(add(block(2), up), add(block(-2), down)))
    up, down = join(*both_ways(add(block(1), up), add(block(-1), down)))
    slope = block(0).astype(F32) + up.astype(F32) + down.astype(F32)
    gvals, uvals = saved[:rows].astype(F32), saved[rows:].astype(F32)
    sig = jax.nn.sigmoid(gvals)
    gate_grad = (slope * uvals * sig * (1.0 + gvals * (1.0 - sig))).astype(BF16)
    up_grad = (slope * gvals * sig).astype(BF16)
    pieces, both = join(jnp.concatenate([gate_grad, up_grad], axis=1), both)
    pieces = lax.all_gather(pieces, "z", axis=0, tiled=True)
    pieces = with_layout_constraint(pieces, Layout(major_to_minor=(0, 1)))

    both = both.astype(F32)
    hidden = (jax.nn.silu(both[:, :cols]) * both[:, cols:]).astype(BF16)
    spots = put(jnp.zeros((8 * rows, cols), BF16), hidden, place(0) * rows)
    up, down = hidden, hidden
    for k in (1, 2, 3):
        up, down = join(*both_ways(up, down))
        spots = put(put(spots, up, place(-k) * rows), down, place(k) * rows)
    up, down = both_ways(up[:, :cut], down[:, cut:])
    spots = put(put(spots, up, place(4) * rows), down, place(4) * rows, cut)
    mixed = reduce_cores(lambda v: dot(v, down_pair), spots[4 * rows:], spots[:4 * rows])
    pieces, mixed = join(pieces, mixed)

    def chosen(core):
        return jnp.concatenate(
            [part(pieces, 2 * ((x + j) % 4) + core, rows, 0) for j in range(4)], axis=0
        )

    mixed = reduce_chips(mixed)
    back = reduce_cores(lambda v: dot_t(v, w_both), *join(chosen(1 - c), chosen(c)))
    back = reduce_chips(back)
    (ends,) = join(jnp.stack([mixed[:, feats:], back[:, feats:]]).astype(BF16))
    ends = shift(ends, "y", 1).astype(F32)
    forward_result = (inputs.astype(F32) + mixed[:, :feats] + ends[0]).astype(BF16)
    backward_result = (grads.astype(F32) + back[:, :feats] + ends[1]).astype(BF16)

    outgoing = jnp.where(lax.axis_index("s") == 0, forward_result, backward_result)
    received = shift(outgoing, "s", 1)
    return (forward_result[None], backward_result[None], received[None])


def solution(mesh):
    fine = Mesh(mesh.devices.reshape(2, 8, 2, 4, 2), ("s", "z", "y", "x", "c"))
    tokens = P("s", ("x", "c"), ("z", "y"))
    hidden = P("s", ("z", "y"), ("x", "c"))
    return jax.shard_map(
        local,
        mesh=fine,
        in_specs=(tokens, tokens, hidden, hidden, hidden, hidden, tokens),
        out_specs=(tokens, tokens, tokens),
        check_vma=False,
    )
```

```python
import jax
import jax.numpy as jnp
from jax import lax
from jax.experimental import pallas as pl
from jax.experimental.pallas import tpu as pltpu
from jax.experimental.layout import Layout, with_layout_constraint
from jax.sharding import Mesh
from jax.sharding import PartitionSpec as P

F32 = jnp.float32
BF16 = jnp.bfloat16


def shift(v, axis, by):
    n = lax.axis_size(axis)
    return lax.ppermute(v, axis, [(i, (i + by) % n) for i in range(n)])


def join(*values):
    return lax.optimization_barrier(values)


def part(v, index, size, dim):
    return lax.dynamic_slice_in_dim(v, index * size, size, dim)


def put(base, piece, row, col=0):
    return lax.dynamic_update_slice(base, piece, (jnp.int32(row), jnp.int32(col)))


def dot(left, right):
    return jnp.dot(left, right, preferred_element_type=F32)


def dot_t(left, right):
    return lax.dot_general(left, right, (((1,), (1,)), ((), ())), preferred_element_type=F32)


def slope_kernel(left_ref, kept_ref, got_ref, out_ref):
    feats = kept_ref.shape[1]
    total = dot_t(left_ref[:, :feats], kept_ref[...]) + dot_t(left_ref[:, feats:], got_ref[...])
    out_ref[...] = total.astype(out_ref.dtype)


def gate_kernel(left_ref, kept_ref, got_ref, out_ref):
    feats = kept_ref.shape[0]
    total = dot(left_ref[:, :feats], kept_ref[...]) + dot(left_ref[:, feats:], got_ref[...])
    out_ref[...] = total.astype(out_ref.dtype)


def product(kernel, tokens, column, kept, got, width, steps, flops):
    m, k = tokens.shape[0], tokens.shape[1] // 2
    half = got.shape
    return pl.pallas_call(
        kernel,
        grid=(steps,),
        in_specs=[
            pl.BlockSpec((m // steps, k), lambda i: (i, column)),
            pl.BlockSpec(half, lambda i: (0, 0)),
            pl.BlockSpec(half, lambda i: (0, 0)),
        ],
        out_specs=pl.BlockSpec((m // steps, width), lambda i: (i, 0)),
        out_shape=jax.ShapeDtypeStruct((m, width), BF16),
        compiler_params=pltpu.CompilerParams(vmem_limit_bytes=60 << 20),
        cost_estimate=pl.CostEstimate(flops=flops, transcendentals=0, bytes_accessed=0),
    )(tokens, kept, got)


def add(left, right):
    return (left.astype(F32) + right.astype(F32)).astype(BF16)


def both_ways(up, down):
    up, down = join(up, down)
    return shift(up, "z", 1), shift(down, "z", -1)


def reduce_cores(product, away, stay):
    return product(stay) + shift(product(away).astype(BF16), "c", 1).astype(F32)


def reduce_chips(v):
    rows = v.shape[0] // 4
    sends = join(*(v[j * rows:(j + 1) * rows].astype(BF16) for j in (2, 1, 3)))
    total = v[:rows]
    for piece, by in zip(sends, (2, 1, -1)):
        total = total + shift(piece, "x", by).astype(F32)
    return total


def local(fwd_in, grad_in, saved_gate, saved_up, gate_weight, up_weight, down_weight):
    inputs = fwd_in[0]
    grads = grad_in[0]
    w_gate, w_up, w_down = gate_weight[0], up_weight[0], down_weight[0]
    z, y = lax.axis_index("z"), lax.axis_index("y")
    x, c = lax.axis_index("x"), lax.axis_index("c")
    rows, feats = inputs.shape
    cols = w_gate.shape[1] // 2
    cut = 4 * cols // 7

    def owner(k):
        return (z + k + 8) % 8

    def place(k):
        return 4 * ((owner(k) + c) % 2) + (owner(k) // 2 + 4 - x) % 4

    tokens = jnp.stack([inputs, grads])
    w_away = jnp.concatenate([part(w_gate, 1 - y, cols, 1), part(w_up, 1 - y, cols, 1)], axis=1)
    tokens_got = shift(tokens, "y", 1)
    tokens_got, w_away = join(tokens_got, w_away)
    tokens = jnp.concatenate([inputs, tokens_got[0], grads, tokens_got[1]], axis=1)
    (tokens,) = join(lax.all_gather(tokens, ("x", "c"), axis=0, tiled=True))
    w_got = shift(w_away, "y", 1)
    down_away = part(w_down, 1 - y, cols, 0)
    w_both = jnp.zeros((2 * feats, 2 * cols), BF16)
    w_both = put(w_both, part(w_gate, y, cols, 1), 0)
    w_both = put(w_both, part(w_up, y, cols, 1), 0, cols)
    down_kept = part(w_down, y, cols, 0)
    saved = jnp.concatenate([saved_gate[0], saved_up[0]], axis=0)
    saved_away, saved = part(saved, 1 - y, cols, 1), part(saved, y, cols, 1)
    w_got, w_both, down_away, down_kept, saved, saved_away = join(
        w_got, w_both, down_away, down_kept, saved, saved_away
    )

    down_got = shift(down_away, "y", 1)
    both = product(gate_kernel, tokens, 0, w_both, w_got, 2 * cols, 4, int(1.5e10))
    ready = both
    both = lax.psum_scatter(both, "z", scatter_dimension=0, tiled=True)
    saved_got = shift(saved_away, "y", 1)
    half = rows // 2
    saved = jnp.where(
        y == 0,
        jnp.concatenate([saved[:half], saved_got[:half], saved[half:], saved_got[half:]]),
        jnp.concatenate([saved_got[:half], saved[:half], saved_got[half:], saved[half:]]),
    )
    down_got, saved, ready, w_got = join(down_got, saved, ready, w_got)
    term = product(slope_kernel, tokens, 1, down_kept, down_got, cols, 2, int(45e9))

    def block(k):
        return part(term, owner(k), rows, 0)

    a = block(4)
    up, down = join(*both_ways(a[:, :cut], a[:, cut:]))
    a, b = block(3), block(-3)
    up = jnp.concatenate([add(a[:, :cut], up), a[:, cut:]], axis=1)
    down = jnp.concatenate([b[:, :cut], add(b[:, cut:], down)], axis=1)
    up, down = join(*both_ways(up, down))
    up, down = join(*both_ways(add(block(2), up), add(block(-2), down)))
    up, down = join(*both_ways(add(block(1), up), add(block(-1), down)))
    slope = block(0).astype(F32) + up.astype(F32) + down.astype(F32)
    gvals, uvals = saved[:rows].astype(F32), saved[rows:].astype(F32)
    sig = jax.nn.sigmoid(gvals)
    gate_grad = (slope * uvals * sig * (1.0 + gvals * (1.0 - sig))).astype(BF16)
    up_grad = (slope * gvals * sig).astype(BF16)
    pieces, both = join(jnp.concatenate([gate_grad, up_grad], axis=1), both)
    pieces = lax.all_gather(pieces, "z", axis=0, tiled=True)
    pieces = with_layout_constraint(pieces, Layout(major_to_minor=(0, 1)))

    both = both.astype(F32)
    hidden = (jax.nn.silu(both[:, :cols]) * both[:, cols:]).astype(BF16)
    spots = put(jnp.zeros((8 * rows, cols), BF16), hidden, place(0) * rows)
    hidden, down_got, w_got = join(hidden, down_got, w_got)
    up, down = hidden, hidden
    for k in (1, 2, 3):
        up, down = both_ways(up, down)
        if k == 1:
            down_pair = jnp.concatenate([down_kept, down_got], axis=1)
            up, down, down_pair, w_got = join(up, down, down_pair, w_got)
        elif k == 2:
            w_both = put(w_both, w_got, feats)
            up, down, w_both = join(up, down, w_both)
        else:
            up, down = join(up, down)
        spots = put(put(spots, up, place(-k) * rows), down, place(k) * rows)
    up, down = both_ways(up[:, :cut], down[:, cut:])
    spots = put(put(spots, up, place(4) * rows), down, place(4) * rows, cut)
    mixed = reduce_cores(lambda v: dot(v, down_pair), spots[4 * rows:], spots[:4 * rows])
    pieces, mixed = join(pieces, mixed)

    def chosen(core):
        return jnp.concatenate(
            [part(pieces, 2 * ((x + j) % 4) + core, rows, 0) for j in range(4)], axis=0
        )

    mixed = reduce_chips(mixed)
    back = reduce_cores(lambda v: dot_t(v, w_both), *join(chosen(1 - c), chosen(c)))
    back = reduce_chips(back)
    (ends,) = join(jnp.stack([mixed[:, feats:], back[:, feats:]]).astype(BF16))
    ends = shift(ends, "y", 1).astype(F32)
    forward_result = (inputs.astype(F32) + mixed[:, :feats] + ends[0]).astype(BF16)
    backward_result = (grads.astype(F32) + back[:, :feats] + ends[1]).astype(BF16)

    outgoing = jnp.where(lax.axis_index("s") == 0, forward_result, backward_result)
    received = shift(outgoing, "s", 1)
    return (forward_result[None], backward_result[None], received[None])


def solution(mesh):
    fine = Mesh(mesh.devices.reshape(2, 8, 2, 4, 2), ("s", "z", "y", "x", "c"))
    tokens = P("s", ("x", "c"), ("z", "y"))
    hidden = P("s", ("z", "y"), ("x", "c"))
    return jax.shard_map(
        local,
        mesh=fine,
        in_specs=(tokens, tokens, hidden, hidden, hidden, hidden, tokens),
        out_specs=(tokens, tokens, tokens),
        check_vma=False,
    )
```

```python
import jax
import jax.numpy as jnp
from jax import lax
from jax.experimental import pallas as pl
from jax.experimental.pallas import tpu as pltpu
from jax.experimental.layout import Layout, with_layout_constraint
from jax.sharding import Mesh
from jax.sharding import PartitionSpec as P

F32 = jnp.float32
BF16 = jnp.bfloat16


def shift(v, axis, by):
    n = lax.axis_size(axis)
    return lax.ppermute(v, axis, [(i, (i + by) % n) for i in range(n)])


def join(*values):
    return lax.optimization_barrier(values)


def part(v, index, size, dim):
    return lax.dynamic_slice_in_dim(v, index * size, size, dim)


def put(base, piece, row, col=0):
    return lax.dynamic_update_slice(base, piece, (jnp.int32(row), jnp.int32(col)))


def dot(left, right):
    return jnp.dot(left, right, preferred_element_type=F32)


def dot_t(left, right):
    return lax.dot_general(left, right, (((1,), (1,)), ((), ())), preferred_element_type=F32)


def slope_kernel(left_ref, kept_ref, got_ref, out_ref):
    feats = kept_ref.shape[1]
    total = dot_t(left_ref[:, :feats], kept_ref[...]) + dot_t(left_ref[:, feats:], got_ref[...])
    out_ref[...] = total.astype(out_ref.dtype)


def gate_kernel(left_ref, kept_ref, got_ref, out_ref):
    feats = kept_ref.shape[0]
    total = dot(left_ref[:, :feats], kept_ref[...]) + dot(left_ref[:, feats:], got_ref[...])
    out_ref[...] = total.astype(out_ref.dtype)


def product(kernel, tokens, column, kept, got, width, steps, flops):
    m, k = tokens.shape[0], tokens.shape[1] // 2
    half = got.shape
    return pl.pallas_call(
        kernel,
        grid=(steps,),
        in_specs=[
            pl.BlockSpec((m // steps, k), lambda i: (i, column)),
            pl.BlockSpec(half, lambda i: (0, 0)),
            pl.BlockSpec(half, lambda i: (0, 0)),
        ],
        out_specs=pl.BlockSpec((m // steps, width), lambda i: (i, 0)),
        out_shape=jax.ShapeDtypeStruct((m, width), BF16),
        compiler_params=pltpu.CompilerParams(vmem_limit_bytes=60 << 20),
        cost_estimate=pl.CostEstimate(flops=flops, transcendentals=0, bytes_accessed=0),
    )(tokens, kept, got)


def add(left, right):
    return (left.astype(F32) + right.astype(F32)).astype(BF16)


def both_ways(up, down):
    up, down = join(up, down)
    return shift(up, "z", 1), shift(down, "z", -1)


def reduce_cores(product, away, stay):
    return product(stay) + shift(product(away).astype(BF16), "c", 1).astype(F32)


def reduce_chips(v):
    rows = v.shape[0] // 4
    sends = join(*(v[j * rows:(j + 1) * rows].astype(BF16) for j in (2, 1, 3)))
    total = v[:rows]
    for piece, by in zip(sends, (2, 1, -1)):
        total = total + shift(piece, "x", by).astype(F32)
    return total


def local(fwd_in, grad_in, saved_gate, saved_up, gate_weight, up_weight, down_weight):
    inputs = fwd_in[0]
    grads = grad_in[0]
    w_gate, w_up, w_down = gate_weight[0], up_weight[0], down_weight[0]
    z, y = lax.axis_index("z"), lax.axis_index("y")
    x, c = lax.axis_index("x"), lax.axis_index("c")
    rows, feats = inputs.shape
    cols = w_gate.shape[1] // 2
    cut = 4 * cols // 7

    def owner(k):
        return (z + k + 8) % 8

    def place(k):
        return 4 * ((owner(k) + c) % 2) + (owner(k) // 2 + 4 - x) % 4

    tokens = jnp.stack([inputs, grads])
    w_away = jnp.concatenate([part(w_gate, 1 - y, cols, 1), part(w_up, 1 - y, cols, 1)], axis=1)
    tokens_got = shift(tokens, "y", 1)
    tokens_got, w_away = join(tokens_got, w_away)
    tokens = jnp.concatenate([inputs, tokens_got[0], grads, tokens_got[1]], axis=1)
    (tokens,) = join(lax.all_gather(tokens, ("x", "c"), axis=0, tiled=True))
    w_got = shift(w_away, "y", 1)
    down_away = part(w_down, 1 - y, cols, 0)
    w_both = jnp.zeros((2 * feats, 2 * cols), BF16)
    w_both = put(w_both, part(w_gate, y, cols, 1), 0)
    w_both = put(w_both, part(w_up, y, cols, 1), 0, cols)
    down_kept = part(w_down, y, cols, 0)
    saved = jnp.concatenate([saved_gate[0], saved_up[0]], axis=0)
    saved_away, saved = part(saved, 1 - y, cols, 1), part(saved, y, cols, 1)
    w_got, w_both, down_away, down_kept, saved, saved_away = join(
        w_got, w_both, down_away, down_kept, saved, saved_away
    )

    down_got = shift(down_away, "y", 1)
    both = product(gate_kernel, tokens, 0, w_both, w_got, 2 * cols, 4, int(1.5e10))
    ready = both
    both = lax.psum_scatter(both, "z", scatter_dimension=0, tiled=True)
    saved_got = shift(saved_away, "y", 1)
    half = rows // 2
    saved = jnp.where(
        y == 0,
        jnp.concatenate([saved[:half], saved_got[:half], saved[half:], saved_got[half:]]),
        jnp.concatenate([saved_got[:half], saved[:half], saved_got[half:], saved[half:]]),
    )
    down_got, saved, ready, w_got = join(down_got, saved, ready, w_got)
    term = product(slope_kernel, tokens, 1, down_kept, down_got, cols, 2, int(4e10))

    def block(k):
        return part(term, owner(k), rows, 0)

    a = block(4)
    up, down = both_ways(a[:, :cut], a[:, cut:])
    down_pair = jnp.concatenate([down_kept, down_got], axis=1)
    w_both = put(w_both, w_got, feats)
    up, down, down_pair, w_both = join(up, down, down_pair, w_both)
    a, b = block(3), block(-3)
    up = jnp.concatenate([add(a[:, :cut], up), a[:, cut:]], axis=1)
    down = jnp.concatenate([b[:, :cut], add(b[:, cut:], down)], axis=1)
    up, down = join(*both_ways(up, down))
    up, down = join(*both_ways(add(block(2), up), add(block(-2), down)))
    up, down = join(*both_ways(add(block(1), up), add(block(-1), down)))
    slope = block(0).astype(F32) + up.astype(F32) + down.astype(F32)
    gvals, uvals = saved[:rows].astype(F32), saved[rows:].astype(F32)
    sig = jax.nn.sigmoid(gvals)
    gate_grad = (slope * uvals * sig * (1.0 + gvals * (1.0 - sig))).astype(BF16)
    up_grad = (slope * gvals * sig).astype(BF16)
    pieces, both = join(jnp.concatenate([gate_grad, up_grad], axis=1), both)
    pieces = lax.all_gather(pieces, "z", axis=0, tiled=True)
    pieces = with_layout_constraint(pieces, Layout(major_to_minor=(0, 1)))

    both = both.astype(F32)
    hidden = (jax.nn.silu(both[:, :cols]) * both[:, cols:]).astype(BF16)
    spots = put(jnp.zeros((8 * rows, cols), BF16), hidden, place(0) * rows)
    up, down = hidden, hidden
    for k in (1, 2, 3):
        up, down = join(*both_ways(up, down))
        spots = put(put(spots, up, place(-k) * rows), down, place(k) * rows)
    up, down = both_ways(up[:, :cut], down[:, cut:])
    spots = put(put(spots, up, place(4) * rows), down, place(4) * rows, cut)
    mixed = reduce_cores(lambda v: dot(v, down_pair), spots[4 * rows:], spots[:4 * rows])
    pieces, mixed = join(pieces, mixed)

    def chosen(core):
        return jnp.concatenate(
            [part(pieces, 2 * ((x + j) % 4) + core, rows, 0) for j in range(4)], axis=0
        )

    mixed = reduce_chips(mixed)
    back = reduce_cores(lambda v: dot_t(v, w_both), *join(chosen(1 - c), chosen(c)))
    back = reduce_chips(back)
    (ends,) = join(jnp.stack([mixed[:, feats:], back[:, feats:]]).astype(BF16))
    ends = shift(ends, "y", 1).astype(F32)
    forward_result = (inputs.astype(F32) + mixed[:, :feats] + ends[0]).astype(BF16)
    backward_result = (grads.astype(F32) + back[:, :feats] + ends[1]).astype(BF16)

    outgoing = jnp.where(lax.axis_index("s") == 0, forward_result, backward_result)
    received = shift(outgoing, "s", 1)
    return (forward_result[None], backward_result[None], received[None])


def solution(mesh):
    fine = Mesh(mesh.devices.reshape(2, 8, 2, 4, 2), ("s", "z", "y", "x", "c"))
    tokens = P("s", ("x", "c"), ("z", "y"))
    hidden = P("s", ("z", "y"), ("x", "c"))
    return jax.shard_map(
        local,
        mesh=fine,
        in_specs=(tokens, tokens, hidden, hidden, hidden, hidden, tokens),
        out_specs=(tokens, tokens, tokens),
        check_vma=False,
    )
```
